128 devices in a mesh: dp: 32 (over y_hi, z, x), tensor: 4 (over y_lo, core).
Axes of the slice: x: 4, y: 4 (y_hi: 2, y_lo: 2; y = y_hi * 2 + y_lo), z: 4, core: 2. Of those that a mesh axis runs over, the one named last changes fastest.
Arguments:
- hidden_in: float32 [16384, 1024], P(('dp', 'tensor')), may hold values from -6 to 6
- segments: int32 [32, 512], P('dp'), may hold values from 0 to 3, never falling along the last dimension, each value on 1 to 256 neighbouring positions
- w_qkv: bfloat16 [2, 1024, 3, 1024], P(None, 'dp', None, 'tensor'), may hold values from -0.1875 to 0.1875
- w_out: bfloat16 [2, 1024, 1024], P(None, 'dp', 'tensor'), may hold values from -0.75 to 0.75
- w_up: bfloat16 [2, 1024, 4096], P(None, 'dp', 'tensor'), may hold values from -0.1875 to 0.1875
- w_down: bfloat16 [2, 1024, 4096], P(None, 'dp', 'tensor'), may hold values from -0.09375 to 0.09375
- qv_bias: float32 [2, 2, 1024], replicated, may hold values from -2 to 2
- proj_bias: float32 [2, 2, 1024], replicated, may hold values from -2 to 2
- up_bias: float32 [2, 4096], replicated, may hold values from -3 to 3
- ln_gain: float32 [2, 2, 1024], replicated, may hold values from 0.5 to 1.5
- ln_shift: float32 [2, 2, 1024], replicated, may hold values from -2 to 2
- cotangent: float32 [16384, 1024], P(('dp', 'tensor')), may hold values from -6 to 6
Outputs:
- layer_out: float32 [16384, 1024], P(('dp', 'tensor'))
- grad_in: float32 [16384, 1024], P(('dp', 'tensor'))
- grad_qkv: float32 [2, 1024, 3, 1024], P(None, 'dp', None, 'tensor')
- grad_out: float32 [2, 1024, 1024], P(None, 'dp', 'tensor')
- grad_up: float32 [2, 1024, 4096], P(None, 'dp', 'tensor')
- grad_down: float32 [2, 1024, 4096], P(None, 'dp', 'tensor')
- grad_qv_bias: float32 [2, 2, 1024], replicated
- grad_proj_bias: float32 [2, 2, 1024], replicated
- grad_up_bias: float32 [2, 4096], replicated
- grad_ln_gain: float32 [2, 2, 1024], replicated
- grad_ln_shift: float32 [2, 2, 1024], replicated
The draws below stay inside these ranges and needn't reach their ends.
Inputs may be any that keep to these rules, and one draw needn't show every extreme that they name: `segments`: in each sequence the document numbers never fall; every document holds 1 to 256 tokens and one holds exactly 256.
All inputs are finite; a program needn't handle non-finite values.
Results may differ from the reference program's by a relative error of at most 0.025.
Values may be sent and summed in bfloat16 or wider, within the bound.
No kernel may reach another device: no remote copies, remote signals or barrier semaphores. Data moves between devices by JAX's collectives and lax.ppermute only.
A program may use at most 128 MiB of HBM per device.

```python
import math
import jax
import jax.numpy as jnp
import numpy as np
from jax import lax

D = 1024
HEADS = 16
HEAD_DIM = 64
FF = 4096
LAYERS = 2
SEQ_LEN = 512
DOCS = 4
DOC_MOST = 256
SEQS = 32
TOKENS = 16384


def steps_of(key, shape, split, low, top_value):
    def one(dim, blocks):
        heights = jax.random.uniform(jax.random.fold_in(jax.random.fold_in(key, 6), dim), (blocks,), jnp.float32, low / len(split), top_value / len(split))
        return jnp.repeat(jnp.exp(heights), shape[dim] // blocks).reshape((-1,) + (1,) * (len(shape) - dim - 1))

    loudness = one(*split[0])
    for cut in split[1:]:
        loudness = loudness * one(*cut)
    return loudness


def split_up(count, total, bound, skew):
    loads = [(1 << 20) // math.isqrt(rank ** skew) + 1 for rank in range(2, count + 1)]
    surplus, given = total - bound - (count - 1), [1] * (count - 1)
    while surplus > 0:
        free = [i for i in range(count - 1) if given[i] < bound]
        pool, budget = sum([loads[i] for i in free]), surplus
        for i in free:
            more = min(bound - given[i], max(1, budget * loads[i] // pool), surplus)
            given[i] = given[i] + more
            surplus = surplus - more
    return np.array([bound] + given)


def ragged(key, count, total, most, slope):
    if count == 2:
        one = jax.random.randint(key, (), max(1, total - most), min(most, total - 1) + 1)
        return jnp.stack([one, total - one])
    sizes = jnp.asarray(split_up(count, total, most, slope), jnp.int32)
    pairs = (count - 1) // 2
    source_of, receiver = sizes[1:1 + 2 * pairs:2], sizes[2:2 + 2 * pairs:2]
    margin = jnp.minimum(source_of - 1, most - receiver)
    moved = jax.random.randint(jax.random.fold_in(key, 1), (pairs,), 0, 1 << 20) % (margin + 1)
    sizes = sizes.at[1:1 + 2 * pairs:2].set(source_of - moved).at[2:2 + 2 * pairs:2].set(receiver + moved)
    return sizes[jax.random.permutation(jax.random.fold_in(key, 2), count)]


def centred(rng, dims, scale, bound, cuts=(), dtype=jnp.bfloat16):
    array = scale * jax.random.normal(rng, dims, jnp.float32)
    if cuts:
        array = array * steps_of(rng, dims, cuts, -0.22, 0.18)
    return jnp.clip(array, -bound, bound).astype(dtype)


def setup_inputs(seed: int = 0) -> dict:
    streams_of = jax.random.split(jax.random.key(seed), 13)
    hidden_in = centred(streams_of[0], (TOKENS, D), 1.0, 6.0, ((0, 128),), jnp.float32)
    segments = jax.vmap(lambda own: jnp.searchsorted(jnp.cumsum(ragged(own, DOCS, SEQ_LEN, DOC_MOST, 2)), jnp.arange(SEQ_LEN), side="right"))(jax.random.split(streams_of[1], SEQS)).reshape((SEQS, SEQ_LEN)).astype(jnp.int32)
    w_qkv = centred(streams_of[2], (LAYERS, D, 3, D), D ** -0.5, 0.1875, ((1, 32), (3, 4)))
    w_out = centred(streams_of[3], (LAYERS, D, D), (D // 16) ** -0.5, 0.75, ((1, 32), (2, 4)))
    w_up = centred(streams_of[4], (LAYERS, D, FF), D ** -0.5, 0.1875, ((1, 32), (2, 4)))
    w_down = centred(streams_of[5], (LAYERS, D, FF), FF ** -0.5, 0.09375, ((1, 32), (2, 4)))
    qv_bias = centred(streams_of[6], (LAYERS, 2, D), 0.3, 2.0, (), jnp.float32)
    proj_bias = centred(streams_of[7], (LAYERS, 2, D), 0.3, 2.0, (), jnp.float32)
    up_bias = centred(streams_of[8], (LAYERS, FF), 0.5, 3.0, (), jnp.float32)
    ln_gain = jnp.clip(1.0 + 0.1 * jax.random.normal(streams_of[9], (LAYERS, 2, D), jnp.float32), 0.5, 1.5)
    ln_shift = centred(streams_of[10], (LAYERS, 2, D), 0.3, 2.0, (), jnp.float32)
    cotangent = centred(streams_of[11], (TOKENS, D), 1.0, 6.0, ((0, 128),), jnp.float32)
    return dict(hidden_in=hidden_in, segments=segments, w_qkv=w_qkv, w_out=w_out, w_up=w_up, w_down=w_down, qv_bias=qv_bias, proj_bias=proj_bias, up_bias=up_bias, ln_gain=ln_gain, ln_shift=ln_shift, cotangent=cotangent)


NORM_EPS = 1e-12
HALF_ROOT = 0.7071067811865476
DENSITY = 0.3989422804014327

def normal_cdf(values):
    return 0.5 * (1.0 + lax.erf(values * HALF_ROOT))

def gelu_slope(values):
    return normal_cdf(values) + values * jnp.exp(-0.5 * values * values) * DENSITY

def layer_norm(activations, gain_row, shift_row):
    center = activations - lax.optimization_barrier(jnp.mean(activations, axis=-1, keepdims=True))
    inv_std = lax.rsqrt(lax.optimization_barrier(jnp.mean(center * center, axis=-1, keepdims=True)) + NORM_EPS)
    normed = center * inv_std
    return (normed * gain_row + shift_row, normed, inv_std)

def norm_back(upstream, normed, inv_std, gain_row):
    scaled = upstream * gain_row
    return inv_std * (scaled - lax.optimization_barrier(jnp.mean(scaled, axis=-1, keepdims=True)) - normed * lax.optimization_barrier(jnp.mean(scaled * normed, axis=-1, keepdims=True)))

def masked_scores(query_heads, key_heads, seg_ids):
    raw_scores = jnp.einsum('qhe,khe->hqk', query_heads.astype(jnp.float32), key_heads.astype(jnp.float32))
    scores = raw_scores * (1.0 / math.sqrt(HEAD_DIM))
    same_doc = seg_ids[:, None] == seg_ids[None, :]
    return jnp.where(same_doc[None, :, :], scores, -jnp.inf)

def attend(packed):
    head_view, seg_ids = packed
    scores = masked_scores(head_view[:, 0], head_view[:, 1], seg_ids)
    row_peak = lax.optimization_barrier(jnp.max(scores, axis=-1, keepdims=True))
    log_total = row_peak + jnp.log(lax.optimization_barrier(jnp.sum(jnp.exp(scores - row_peak), axis=-1, keepdims=True)))
    attn_probs = jnp.exp(scores - log_total).astype(jnp.bfloat16)
    context = jnp.einsum('hqk,khe->qhe', attn_probs.astype(jnp.float32), head_view[:, 2].astype(jnp.float32)).astype(jnp.bfloat16)
    return (context, log_total)

def attend_back(packed):
    head_view, seg_ids, log_total, grad_context = packed
    query_heads = head_view[:, 0]
    key_heads = head_view[:, 1]
    value_heads = head_view[:, 2]
    scores = masked_scores(query_heads, key_heads, seg_ids)
    attn_probs = jnp.exp(scores - log_total)
    probs_bf = attn_probs.astype(jnp.bfloat16)
    grad_f = grad_context.astype(jnp.float32)
    grad_probs = jnp.einsum('qhe,khe->hqk', grad_f, value_heads.astype(jnp.float32))
    grad_value = jnp.einsum('hqk,qhe->khe', probs_bf.astype(jnp.float32), grad_f)
    row_dot = lax.optimization_barrier(jnp.sum(attn_probs * grad_probs, axis=-1, keepdims=True))
    grad_scores = (attn_probs * (grad_probs - row_dot) * (1.0 / math.sqrt(HEAD_DIM))).astype(jnp.bfloat16)
    grad_scores_f = grad_scores.astype(jnp.float32)
    grad_query = jnp.einsum('hqk,khe->qhe', grad_scores_f, key_heads.astype(jnp.float32))
    grad_key = jnp.einsum('hqk,qhe->khe', grad_scores_f, query_heads.astype(jnp.float32))
    return jnp.stack([grad_query, grad_key, grad_value], axis=1)

def reference(hidden_in, segments, w_qkv, w_out, w_up, w_down, qv_bias, proj_bias, up_bias, ln_gain, ln_shift, cotangent):
    single = jnp.float32
    bfloat = jnp.bfloat16
    tokens = hidden_in.shape[0]
    current = hidden_in
    stored = []
    for layer_index in range(LAYERS):
        inputs_bf = current.astype(bfloat)
        mixed_rows = jnp.dot(inputs_bf, w_qkv[layer_index].reshape(D, 3 * D), preferred_element_type=single).reshape(tokens, 3, D)
        bias_three = jnp.stack([qv_bias[layer_index, 0], jnp.zeros((D,), single), qv_bias[layer_index, 1]])
        qkv_bf = (mixed_rows + bias_three).astype(bfloat)
        head_view = qkv_bf.reshape(SEQS, SEQ_LEN, 3, HEADS, HEAD_DIM)
        context, log_total = lax.map(attend, (head_view, segments))
        context_rows = context.reshape(tokens, D)
        attn_full = jnp.dot(context_rows, w_out[layer_index].T, preferred_element_type=single)
        resid_one = current + attn_full + proj_bias[layer_index, 0]
        middle, normed_one, inv_one = layer_norm(resid_one, ln_gain[layer_index, 0], ln_shift[layer_index, 0])
        middle_bf = middle.astype(bfloat)
        hidden_pre = jnp.dot(middle_bf, w_up[layer_index], preferred_element_type=single) + up_bias[layer_index]
        hidden_bf = (hidden_pre * normal_cdf(hidden_pre)).astype(bfloat)
        down_full = jnp.dot(hidden_bf, w_down[layer_index].T, preferred_element_type=single)
        resid_two = middle + down_full + proj_bias[layer_index, 1]
        output_rows, normed_two, inv_two = layer_norm(resid_two, ln_gain[layer_index, 1], ln_shift[layer_index, 1])
        stored.append((inputs_bf, qkv_bf, log_total, context_rows, normed_one, inv_one, middle_bf, hidden_pre, hidden_bf, normed_two, inv_two))
        current = output_rows
    final_out = current
    upstream = cotangent
    grads_qkv, grads_out, grads_up, grads_down = ([], [], [], [])
    grads_qv, grads_proj, grads_upb, grads_gain, grads_shift = ([], [], [], [], [])
    for layer_index in reversed(range(LAYERS)):
        inputs_bf, qkv_bf, log_total, context_rows, normed_one, inv_one, middle_bf, hidden_pre, hidden_bf, normed_two, inv_two = stored[layer_index]
        gain_two = lax.optimization_barrier(jnp.sum(upstream * normed_two, axis=0))
        shift_two = lax.optimization_barrier(jnp.sum(upstream, axis=0))
        grad_two = norm_back(upstream, normed_two, inv_two, ln_gain[layer_index, 1])
        bias_two = lax.optimization_barrier(jnp.sum(grad_two, axis=0))
        grad_two_bf = grad_two.astype(bfloat)
        grad_hidden = jnp.dot(grad_two_bf, w_down[layer_index], preferred_element_type=single)
        grad_pre = grad_hidden * gelu_slope(hidden_pre)
        grad_pre_bf = grad_pre.astype(bfloat)
        up_term = lax.optimization_barrier(jnp.sum(grad_pre, axis=0))
        grad_mid = grad_two + jnp.dot(grad_pre_bf, w_up[layer_index].T, preferred_element_type=single)
        gain_one = lax.optimization_barrier(jnp.sum(grad_mid * normed_one, axis=0))
        shift_one = lax.optimization_barrier(jnp.sum(grad_mid, axis=0))
        grad_one = norm_back(grad_mid, normed_one, inv_one, ln_gain[layer_index, 0])
        bias_one = lax.optimization_barrier(jnp.sum(grad_one, axis=0))
        grad_one_bf = grad_one.astype(bfloat)
        grad_context = jnp.dot(grad_one_bf, w_out[layer_index], preferred_element_type=single).astype(bfloat)
        head_view = qkv_bf.reshape(SEQS, SEQ_LEN, 3, HEADS, HEAD_DIM)
        grad_heads = lax.map(attend_back, (head_view, segments, log_total, grad_context.reshape(SEQS, SEQ_LEN, HEADS, HEAD_DIM)))
        grad_mixed = grad_heads.reshape(tokens, 3, D)
        bias_qv = jnp.stack([lax.optimization_barrier(jnp.sum(grad_mixed[:, 0], axis=0)), lax.optimization_barrier(jnp.sum(grad_mixed[:, 2], axis=0))])
        grad_mixed_bf = grad_mixed.astype(bfloat).reshape(tokens, 3 * D)
        grads_qkv.append(jnp.dot(inputs_bf.T, grad_mixed_bf, preferred_element_type=single).reshape(D, 3, D))
        grads_out.append(jnp.dot(grad_one_bf.T, context_rows, preferred_element_type=single))
        grads_up.append(jnp.dot(middle_bf.T, grad_pre_bf, preferred_element_type=single))
        grads_down.append(jnp.dot(grad_two_bf.T, hidden_bf, preferred_element_type=single))
        grads_qv.append(bias_qv)
        grads_proj.append(jnp.stack([bias_one, bias_two]))
        grads_upb.append(up_term)
        grads_gain.append(jnp.stack([gain_one, gain_two]))
        grads_shift.append(jnp.stack([shift_one, shift_two]))
        upstream = grad_one + jnp.dot(grad_mixed_bf, w_qkv[layer_index].reshape(D, 3 * D).T, preferred_element_type=single)
    return (final_out, upstream, jnp.stack(grads_qkv[::-1]), jnp.stack(grads_out[::-1]), jnp.stack(grads_up[::-1]), jnp.stack(grads_down[::-1]), jnp.stack(grads_qv[::-1]), jnp.stack(grads_proj[::-1]), jnp.stack(grads_upb[::-1]), jnp.stack(grads_gain[::-1]), jnp.stack(grads_shift[::-1]))
```

```python
import math

import jax
import jax.numpy as jnp
from jax import lax
from jax.sharding import PartitionSpec as P

HEADS = 16
HEAD_DIM = 64
LAYERS = 2


NORM_EPS = 1e-12
HALF_ROOT = 0.7071067811865476
DENSITY = 0.3989422804014327


def normal_cdf(values):
    return 0.5 * (1.0 + lax.erf(values * HALF_ROOT))


def gelu_slope(values):
    return normal_cdf(values) + values * jnp.exp(-0.5 * values * values) * DENSITY


def layer_norm(activations, gain_row, shift_row):
    center = activations - jnp.mean(activations, axis=-1, keepdims=True)
    inv_std = lax.rsqrt(jnp.mean(center * center, axis=-1, keepdims=True) + NORM_EPS)
    normed = center * inv_std
    return (normed * gain_row + shift_row, normed, inv_std)


def norm_back(upstream, normed, inv_std, gain_row):
    scaled = upstream * gain_row
    return inv_std * (
        scaled
        - jnp.mean(scaled, axis=-1, keepdims=True)
        - normed * jnp.mean(scaled * normed, axis=-1, keepdims=True)
    )


def masked_scores(query_heads, key_heads, seg_ids):
    raw_scores = jnp.einsum(
        "qhe,khe->hqk", query_heads, key_heads, preferred_element_type=jnp.float32
    )
    scores = raw_scores * (1.0 / math.sqrt(HEAD_DIM))
    same_doc = seg_ids[:, None] == seg_ids[None, :]
    return jnp.where(same_doc[None, :, :], scores, -jnp.inf)


def attend(query_heads, key_heads, value_heads, seg_ids):
    scores = masked_scores(query_heads, key_heads, seg_ids)
    row_peak = jnp.max(scores, axis=-1, keepdims=True)
    log_total = row_peak + jnp.log(jnp.sum(jnp.exp(scores - row_peak), axis=-1, keepdims=True))
    attn_probs = jnp.exp(scores - log_total).astype(jnp.bfloat16)
    context = jnp.einsum(
        "hqk,khe->qhe", attn_probs, value_heads, preferred_element_type=jnp.float32
    )
    return (context.astype(jnp.bfloat16), log_total)


def attend_back(query_heads, key_heads, value_heads, seg_ids, log_total, grad_context):
    scores = masked_scores(query_heads, key_heads, seg_ids)
    attn_probs = jnp.exp(scores - log_total)
    probs_bf = attn_probs.astype(jnp.bfloat16)
    grad_probs = jnp.einsum(
        "qhe,khe->hqk", grad_context, value_heads, preferred_element_type=jnp.float32
    )
    grad_value = jnp.einsum(
        "hqk,qhe->khe", probs_bf, grad_context, preferred_element_type=jnp.float32
    )
    row_dot = jnp.sum(attn_probs * grad_probs, axis=-1, keepdims=True)
    grad_scores = (attn_probs * (grad_probs - row_dot) * (1.0 / math.sqrt(HEAD_DIM))).astype(
        jnp.bfloat16
    )
    grad_query = jnp.einsum(
        "hqk,khe->qhe", grad_scores, key_heads, preferred_element_type=jnp.float32
    )
    grad_key = jnp.einsum(
        "hqk,qhe->khe", grad_scores, query_heads, preferred_element_type=jnp.float32
    )
    return jnp.stack([grad_query, grad_key, grad_value], axis=1)


def right_product(left_side, right_side):
    return lax.dot_general(
        left_side, right_side, (((1,), (1,)), ((), ())), preferred_element_type=jnp.float32
    )


RING = 4
GROUPS = 2


def dp_index(outer, depth, across):
    return (outer * RING + depth) * RING + across


def dp_perm(move):
    return [
        (dp_index(outer, depth, across), dp_index(*move(outer, depth, across)))
        for outer in range(GROUPS)
        for depth in range(RING)
        for across in range(RING)
    ]


def shift(block, axis, step):
    if axis == "x":
        perm = dp_perm(lambda o, d, a: (o, d, (a + step) % RING))
    else:
        perm = dp_perm(lambda o, d, a: (o, (d + step) % RING, a))
    return lax.ppermute(block, "dp", perm)


def swap_ring(block, axis, mask):
    if axis == "x":
        perm = dp_perm(lambda o, d, a: (o, d, a ^ mask))
    else:
        perm = dp_perm(lambda o, d, a: (o, d ^ mask, a))
    return lax.ppermute(block, "dp", perm)


def swap_outer(block):
    return lax.ppermute(block, "dp", dp_perm(lambda o, d, a: (1 - o, d, a)))


def swap_tensor(block, mask):
    return lax.ppermute(block, "tensor", [(t, t ^ mask) for t in range(4)])


def ring_gather(block, axis, place, dim):
    from_left = shift(block, axis, 1)
    from_right = shift(block, axis, -1)
    far_first = shift(from_left[:1], axis, 1)
    far_second = shift(from_right[1:], axis, -1)
    far = jnp.concatenate([far_first, far_second], axis=0)
    full = jnp.zeros(block.shape[:dim] + (RING,) + block.shape[dim:], block.dtype)
    for offset, piece in ((0, block), (3, from_left), (1, from_right), (2, far)):
        full = lax.dynamic_update_index_in_dim(full, piece, (place + offset) % RING, dim)
    return full


def ring_scatter(full, axis, place, dim):
    def take(offset):
        return lax.dynamic_index_in_dim(full, (place + offset) % RING, dim, keepdims=False)

    single = jnp.float32
    far = take(2)
    got_first = shift(far[:1], axis, 1)
    got_second = shift(far[1:], axis, -1)
    right = take(1)
    left = take(3)
    to_right = jnp.concatenate(
        [(right[:1].astype(single) + got_first.astype(single)).astype(full.dtype), right[1:]]
    )
    to_left = jnp.concatenate(
        [left[:1], (left[1:].astype(single) + got_second.astype(single)).astype(full.dtype)]
    )
    from_left = shift(to_right, axis, 1)
    from_right = shift(to_left, axis, -1)
    return take(0).astype(single) + from_left.astype(single) + from_right.astype(single)


def gather_weight(local, across_first, spots):
    outer, depth, across = spots
    other = swap_outer(local)
    first = jnp.where(outer == 0, local, other)
    second = jnp.where(outer == 0, other, local)
    block = jnp.stack([first, second])
    if across_first:
        block = ring_gather(block, "x", across, 1)
        block = ring_gather(block, "z", depth, 1)
    else:
        block = ring_gather(block, "z", depth, 1)
        block = ring_gather(block, "x", across, 2)
    return block.reshape(GROUPS * RING * RING * local.shape[0], local.shape[1])


def scatter_grad(full, across_first, spots):
    outer, depth, across = spots
    rows = full.shape[0] // (GROUPS * RING * RING)
    block = full.reshape(GROUPS, RING, RING, rows, full.shape[1])
    if across_first:
        block = ring_scatter(block, "x", across, 2).astype(full.dtype)
        block = ring_scatter(block, "z", depth, 1).astype(full.dtype)
    else:
        block = ring_scatter(block, "z", depth, 1).astype(full.dtype)
        block = ring_scatter(block, "x", across, 1).astype(full.dtype)
    mine = lax.dynamic_index_in_dim(block, outer, 0, keepdims=False)
    given = swap_outer(lax.dynamic_index_in_dim(block, 1 - outer, 0, keepdims=False))
    return mine.astype(jnp.float32) + given.astype(jnp.float32)


def sum_all(vector):
    vector = (vector + swap_tensor(vector, 1)) + (swap_tensor(vector, 2) + swap_tensor(vector, 3))
    vector = vector + swap_outer(vector)
    for axis in ("z", "x"):
        vector = (vector + swap_ring(vector, axis, 1)) + (
            swap_ring(vector, axis, 2) + swap_ring(vector, axis, 3)
        )
    return vector


def outer_sum(left_side, right_side):
    return lax.dot_general(
        left_side, right_side, (((0,), (0,)), ((), ())), preferred_element_type=jnp.float32
    ).astype(jnp.bfloat16)


def shards(
    hidden_in,
    segments,
    w_qkv,
    w_out,
    w_up,
    w_down,
    qv_bias,
    proj_bias,
    up_bias,
    ln_gain,
    ln_shift,
    cotangent,
):
    single = jnp.float32
    bfloat = jnp.bfloat16
    model_width = hidden_in.shape[1]
    tensor_count = lax.axis_size("tensor")
    tensor_pos = lax.axis_index("tensor")
    head_count = HEADS // tensor_count
    head_cols = head_count * HEAD_DIM
    hidden_cols = w_up.shape[2]
    seq_count, seq_length = segments.shape
    all_rows = seq_count * seq_length
    rows_here = hidden_in.shape[0]
    dp_pos = lax.axis_index("dp")
    spots = (dp_pos // (RING * RING), (dp_pos // RING) % RING, dp_pos % RING)
    block_ids = tensor_pos ^ jnp.arange(tensor_count)
    segments = jnp.take(
        segments.reshape(seq_count, tensor_count, rows_here // seq_count), block_ids, axis=1
    ).reshape(seq_count, seq_length)

    def gather_rows(local_part):
        across_part = swap_tensor(local_part, 2)
        beside_part = swap_tensor(local_part, 1)
        corner_part = swap_tensor(across_part, 1)
        return jnp.concatenate([local_part, beside_part, across_part, corner_part], axis=0)

    def sum_rows(partial_sum):
        parts = partial_sum.astype(bfloat).reshape(tensor_count, rows_here, model_width)
        near_part = swap_tensor(parts[3], 1)
        own_part = swap_tensor(parts[1], 1)
        leaving = (parts[2].astype(single) + near_part.astype(single)).astype(bfloat)
        arrived = swap_tensor(leaving, 2)
        return (parts[0].astype(single) + own_part.astype(single)) + arrived.astype(single)

    gathered = []
    gate = None
    for layer_index in range(LAYERS):
        qkv_here = w_qkv[layer_index].reshape(-1, 3 * head_cols)
        pieces = (
            qkv_here[:, : 2 * head_cols],
            jnp.concatenate([qkv_here[:, 2 * head_cols :], w_out[layer_index]], axis=1),
        )
        if gate is not None:
            pieces, gate = lax.optimization_barrier((pieces, gate))
        attn_first = gather_weight(pieces[0], True, spots)
        attn_second = gather_weight(pieces[1], False, spots)
        pieces = (w_up[layer_index], w_down[layer_index])
        pieces, (attn_first, attn_second) = lax.optimization_barrier(
            (pieces, (attn_first, attn_second))
        )
        mat_up = gather_weight(pieces[0], True, spots)
        mat_down = gather_weight(pieces[1], False, spots)
        gate = (mat_up, mat_down)
        gathered.append([attn_first, attn_second, mat_up, mat_down])

    current = hidden_in
    kept_weights = []
    stored = []
    for layer_index in range(LAYERS):
        attn_first, attn_second, mat_up, mat_down = gathered[layer_index]
        mat_qkv = jnp.concatenate([attn_first, attn_second[:, :head_cols]], axis=1)
        mat_out = attn_second[:, head_cols:]
        kept_weights.append((mat_qkv, mat_out, mat_up, mat_down))
        rows_all = gather_rows(current.astype(bfloat))
        mixed_rows = jnp.dot(
            rows_all, mat_qkv, preferred_element_type=single
        ).reshape(all_rows, 3, head_cols)
        bias_here = lax.dynamic_slice_in_dim(
            qv_bias[layer_index], tensor_pos * head_cols, head_cols, 1
        )
        bias_three = jnp.stack([bias_here[0], jnp.zeros((head_cols,), single), bias_here[1]])
        qkv_bf = (mixed_rows + bias_three).astype(bfloat)
        head_view = qkv_bf.reshape(seq_count, seq_length, 3, head_count, HEAD_DIM)
        context, log_total = jax.vmap(attend)(
            head_view[:, :, 0], head_view[:, :, 1], head_view[:, :, 2], segments
        )
        context_rows = context.reshape(all_rows, head_cols)
        resid_one = (
            current + sum_rows(right_product(context_rows, mat_out)) + proj_bias[layer_index, 0]
        )
        middle, normed_one, inv_one = layer_norm(
            resid_one, ln_gain[layer_index, 0], ln_shift[layer_index, 0]
        )
        middle_all = gather_rows(middle.astype(bfloat))
        up_here = lax.dynamic_slice_in_dim(
            up_bias[layer_index], tensor_pos * hidden_cols, hidden_cols, 0
        )
        hidden_pre = jnp.dot(middle_all, mat_up, preferred_element_type=single) + up_here
        hidden_bf = (hidden_pre * normal_cdf(hidden_pre)).astype(bfloat)
        resid_two = (
            middle + sum_rows(right_product(hidden_bf, mat_down)) + proj_bias[layer_index, 1]
        )
        output_rows, normed_two, inv_two = layer_norm(
            resid_two, ln_gain[layer_index, 1], ln_shift[layer_index, 1]
        )
        stored.append(
            (
                rows_all,
                qkv_bf,
                log_total,
                context_rows,
                normed_one,
                inv_one,
                middle_all,
                hidden_pre,
                hidden_bf,
                normed_two,
                inv_two,
            )
        )
        current = output_rows
    upstream = cotangent
    layer_grads = []
    small_layers = []
    for layer_index in reversed(range(LAYERS)):
        (
            rows_all,
            qkv_bf,
            log_total,
            context_rows,
            normed_one,
            inv_one,
            middle_all,
            hidden_pre,
            hidden_bf,
            normed_two,
            inv_two,
        ) = stored[layer_index]
        mat_qkv, mat_out, mat_up, mat_down = kept_weights[layer_index]
        gain_two = jnp.sum(upstream * normed_two, axis=0)
        shift_two = jnp.sum(upstream, axis=0)
        grad_two = norm_back(upstream, normed_two, inv_two, ln_gain[layer_index, 1])
        bias_two = jnp.sum(grad_two, axis=0)
        grad_ffn_all = gather_rows(grad_two.astype(bfloat))
        grad_hidden = jnp.dot(grad_ffn_all, mat_down, preferred_element_type=single)
        grad_pre = grad_hidden * gelu_slope(hidden_pre)
        grad_pre_bf = grad_pre.astype(bfloat)
        up_term = jnp.sum(grad_pre, axis=0)
        grad_up = scatter_grad(outer_sum(middle_all, grad_pre_bf), True, spots)
        grad_down = scatter_grad(outer_sum(grad_ffn_all, hidden_bf), False, spots)
        grad_mid = grad_two + sum_rows(right_product(grad_pre_bf, mat_up))
        gain_one = jnp.sum(grad_mid * normed_one, axis=0)
        shift_one = jnp.sum(grad_mid, axis=0)
        grad_one = norm_back(grad_mid, normed_one, inv_one, ln_gain[layer_index, 0])
        bias_one = jnp.sum(grad_one, axis=0)
        grad_attn_all = gather_rows(grad_one.astype(bfloat))
        grad_context = jnp.dot(grad_attn_all, mat_out, preferred_element_type=single).astype(bfloat)
        head_view = qkv_bf.reshape(seq_count, seq_length, 3, head_count, HEAD_DIM)
        grad_heads = jax.vmap(attend_back)(
            head_view[:, :, 0],
            head_view[:, :, 1],
            head_view[:, :, 2],
            segments,
            log_total,
            grad_context.reshape(seq_count, seq_length, head_count, HEAD_DIM),
        )
        grad_mixed = grad_heads.reshape(all_rows, 3, head_cols)
        bias_qv = jnp.sum(grad_mixed[:, 0::2], axis=0)
        grad_mixed_bf = grad_mixed.astype(bfloat).reshape(all_rows, 3 * head_cols)
        head_first = scatter_grad(
            outer_sum(rows_all, grad_mixed_bf[:, : 2 * head_cols]), True, spots
        )
        head_second = scatter_grad(
            jnp.concatenate(
                [
                    outer_sum(rows_all, grad_mixed_bf[:, 2 * head_cols :]),
                    outer_sum(grad_attn_all, context_rows),
                ],
                axis=1,
            ),
            False,
            spots,
        )
        grad_three = jnp.concatenate([head_first, head_second[:, :head_cols]], axis=1)
        layer_grads.insert(
            0,
            (
                grad_three.reshape(-1, 3, head_cols),
                head_second[:, head_cols:],
                grad_up,
                grad_down,
            ),
        )
        wide_qv = lax.dynamic_update_slice(
            jnp.zeros((2, model_width), single), bias_qv, (0, tensor_pos * head_cols)
        )
        wide_up = lax.dynamic_update_slice(
            jnp.zeros((up_bias.shape[1],), single), up_term, (tensor_pos * hidden_cols,)
        )
        small_sums = jnp.concatenate(
            [
                wide_qv,
                jnp.stack([bias_one, bias_two]),
                wide_up.reshape(-1, model_width),
                jnp.stack([gain_one, gain_two]),
                jnp.stack([shift_one, shift_two]),
            ],
            axis=0,
        )
        small_layers.insert(0, sum_all(small_sums))
        input_part = right_product(grad_mixed_bf, mat_qkv)
        upstream = grad_one + sum_rows(input_part)
    totals = jnp.stack(small_layers)
    up_rows = up_bias.shape[1] // model_width
    cut = 4 + up_rows
    small_totals = (
        totals[:, 0:2],
        totals[:, 2:4],
        totals[:, 4:cut].reshape(up_bias.shape),
        totals[:, cut : cut + 2],
        totals[:, cut + 2 : cut + 4],
    )
    return (
        current,
        upstream,
        jnp.stack([layer_part[0] for layer_part in layer_grads]),
        jnp.stack([layer_part[1] for layer_part in layer_grads]),
        jnp.stack([layer_part[2] for layer_part in layer_grads]),
        jnp.stack([layer_part[3] for layer_part in layer_grads]),
        small_totals[0],
        small_totals[1],
        small_totals[2],
        small_totals[3],
        small_totals[4],
    )


def solution(mesh):
    placed = (
        P(("dp", "tensor"), None),
        P("dp", None),
        P(None, "dp", None, "tensor"),
        P(None, "dp", "tensor"),
        P(None, "dp", "tensor"),
        P(None, "dp", "tensor"),
        P(),
        P(),
        P(),
        P(),
        P(),
        P(("dp", "tensor"), None),
    )
    return jax.shard_map(
        shards,
        mesh=mesh,
        in_specs=placed,
        out_specs=(
            P(("dp", "tensor"), None),
            P(("dp", "tensor"), None),
            P(None, "dp", None, "tensor"),
            P(None, "dp", "tensor"),
            P(None, "dp", "tensor"),
            P(None, "dp", "tensor"),
            P(),
            P(),
            P(),
            P(),
            P(),
        ),
        check_vma=False,
    )
```
